256 devices in a mesh: leaf: 8 (over y, core), sub: 32 (over x, z).
Axes of the slice: x: 4, y: 4, z: 8, core: 2. Of those that a mesh axis runs over, the one named last changes fastest.
Arguments:
- points: bfloat16 [1048576, 32], P(('leaf', 'sub')), may hold values from -6 to 6
- vectors: bfloat16 [1048576, 2, 128], P(('leaf', 'sub')), may hold values from -6 to 6
- inv_length: float32 [32], replicated, may hold values from 0.15 to 0.5
- order: int32 [256, 4096], P(('leaf', 'sub')), may hold values from 0 to 4095, each once within a row
- leaf_basis: bfloat16 [2048, 512, 128], P(('leaf', 'sub')), may hold values from -0.25 to 0.25
- leaf_transfer: bfloat16 [2048, 128, 128], P(('leaf', 'sub')), may hold values from -0.5 to 0.5
- level_transfer: bfloat16 [8, 62, 128, 128], P('leaf'), may hold values from -0.5 to 0.5
- near_list: int32 [2048, 3], P(('leaf', 'sub')), may hold values from 0 to 2047, as said below
- near_count: int32 [2048], P(('leaf', 'sub')), may hold values from 1 to 3, as said below
- pair_list: int32 [256, 3], P(('leaf', 'sub')), may hold values from 0 to 255, as said below
- pair_count: int32 [256], P(('leaf', 'sub')), may hold values from 1 to 3, as said below
- pair_coupling: bfloat16 [256, 3, 128, 128], P(('leaf', 'sub')), may hold values from -0.3125 to 0.3125
- top_list: int32 [8, 2], P('leaf'), may hold values from 0 to 7, as said below
- top_coupling: bfloat16 [8, 2, 128, 128], P('leaf'), may hold values from -0.0625 to 0.0625
Outputs:
- product: float32 [1048576, 2, 128], P(('leaf', 'sub'))
The draws below stay inside these ranges and needn't reach their ends.
Inputs may be any that keep to these rules, and one draw needn't show every extreme that they name: `order`: each row is a permutation. `near_list`: entry 0 of a leaf's list is the leaf itself; entries 1 and 2 are, in either order, the leaves just before and just after it in leaf order within its subtree; where one of them does not exist, the other stands in entry 1 and the leaf itself in entry 2. Only the first near_count entries of a list are used; they never repeat a leaf. Some leaf uses all 3. `pair_list`: the entries of a device node are distinct devices of its own subtree whose sub index differs from its own by 1 to 4. Only the first pair_count entries are used. Some device uses all 3. `top_list`: the entries of a subtree are distinct subtrees other than itself.
All inputs are finite; a program needn't handle non-finite values.
Results may differ from the reference program's by a relative error of at most 0.008.
Values may be sent and summed in bfloat16 or wider, within the bound.
No kernel may reach another device: no remote copies, remote signals or barrier semaphores. Data moves between devices by JAX's collectives and lax.ppermute only.
A program may use at most 64 MiB of HBM per device.

```python
import math
import jax
import jax.numpy as jnp
from jax import lax

F = 32
R = 128
NV = 128
LEAF = 512
LPD = 8
KD = 3
REACH = 4
KS = 2
PTS_DEV = 4096
NPTS = 1048576
NLEAVES = 2048
N_LEAF = 8
N_SUB = 32
DEVICES = 256


def near_tables(key):
    devices = N_LEAF * N_SUB
    leaves = devices * LPD
    per_tree = N_SUB * LPD
    leaf_ids = jnp.arange(leaves, dtype=jnp.int32)
    position = leaf_ids % per_tree
    has_before = position > 0
    has_after = position < per_tree - 1
    before_id = jnp.where(has_before, leaf_ids - 1, leaf_ids)
    after_id = jnp.where(has_after, leaf_ids + 1, leaf_ids)
    flipped = jax.random.randint(jax.random.fold_in(key, 11), (leaves,), 0, 2) == 1
    first_side = jnp.where(flipped, after_id, before_id)
    second_side = jnp.where(flipped, before_id, after_id)
    first_ok = jnp.where(flipped, has_after, has_before)
    second_ok = jnp.where(flipped, has_before, has_after)
    entry_one = jnp.where(first_ok, first_side, second_side)
    both_ok = first_ok & second_ok
    entry_two = jnp.where(both_ok, second_side, leaf_ids)
    existing = 1 + (first_ok | second_ok).astype(jnp.int32) + both_ok.astype(jnp.int32)
    link_table = jnp.stack([leaf_ids, entry_one, entry_two], axis=1).astype(jnp.int32)
    device_ids = leaf_ids // LPD
    crowded = jax.random.randint(jax.random.fold_in(key, 12), (devices,), 0, 8) == 0
    chosen_tree = jax.random.randint(jax.random.fold_in(key, 13), (), 0, N_LEAF)
    chosen_sub = jax.random.randint(jax.random.fold_in(key, 14), (), 1, N_SUB - 1)
    chosen_dev = chosen_tree * N_SUB + chosen_sub
    crowded = crowded | (jnp.arange(devices, dtype=jnp.int32) == chosen_dev)
    extra = jax.random.randint(jax.random.fold_in(key, 15), (leaves,), 0, 3)
    light = jnp.minimum(existing, 1 + extra)
    used_count = jnp.where(crowded[device_ids], existing, light).astype(jnp.int32)
    return (link_table, used_count)


def draw_near_list(key, part):
    return near_tables(key)[0]


def draw_near_count(key, part):
    return near_tables(key)[1]


def pair_tables(key):
    devices = N_LEAF * N_SUB
    window_size = 2 * REACH + 1
    device_ids = jnp.arange(devices, dtype=jnp.int32)
    sub_ids = device_ids % N_SUB
    shifts = jnp.arange(window_size, dtype=jnp.int32) - REACH
    target = sub_ids[:, None] + shifts[None, :]
    usable = (target >= 0) & (target < N_SUB) & (shifts[None, :] != 0)
    random_bits = jax.random.randint(jax.random.fold_in(key, 21), (devices, window_size), 0, 1 << 20)
    scores = jnp.where(usable, random_bits * window_size + jnp.arange(window_size, dtype=jnp.int32)[None, :], -1)
    winners = lax.top_k(scores, KD)[1]
    link_table = (device_ids[:, None] + shifts[winners]).astype(jnp.int32)
    used_count = jax.random.randint(jax.random.fold_in(key, 22), (devices,), 1, KD + 1)
    chosen_dev = jax.random.randint(jax.random.fold_in(key, 23), (), 0, devices)
    used_count = jnp.where(device_ids == chosen_dev, KD, used_count).astype(jnp.int32)
    return (link_table, used_count)


def draw_pair_list(key, part):
    return pair_tables(key)[0]


def draw_pair_count(key, part):
    return pair_tables(key)[1]


def draw_top_list(key, part):
    tree_ids = jnp.arange(N_LEAF, dtype=jnp.int32)
    random_bits = jax.random.randint(jax.random.fold_in(key, 31), (N_LEAF, N_LEAF), 0, 1 << 20)
    scores = jnp.where(tree_ids[:, None] != tree_ids[None, :], random_bits * N_LEAF + tree_ids[None, :], -1)
    return lax.top_k(scores, KS)[1].astype(jnp.int32)


def block_scale(rng, dims, shards, smallest, largest):
    gain, own = 1.0, jax.random.fold_in(rng, 6)
    for dim, shards_of in shards:
        draws = jnp.exp(jax.random.uniform(jax.random.fold_in(own, dim), (shards_of,), jnp.float32, smallest / len(shards), largest / len(shards)))
        gain = gain * jnp.repeat(draws, dims[dim] // shards_of).reshape([-1 if axis == dim else 1 for axis in range(len(dims))])
    return gain


def gaussian(rng, dims, spread, most, cuts=(), held_as=jnp.bfloat16):
    drawn = jax.random.normal(rng, dims, jnp.float32) * spread
    if len(cuts) > 0:
        drawn = block_scale(rng, dims, cuts, -0.22, 0.18) * drawn
    return jnp.clip(drawn, min=-most, max=most).astype(held_as)


def setup_inputs(seed: int = 0) -> dict:
    keys = jax.random.split(jax.random.key(seed), 15)
    return {
        "points": gaussian(keys[0], (NPTS, F), 1.0, 6.0, ((0, 256),)),
        "vectors": gaussian(keys[1], (NPTS, 2, NV), 1.0, 6.0, ((0, 256),)),
        "inv_length": jnp.clip(jnp.exp(jax.random.uniform(keys[2], (F,), jnp.float32, math.log(0.15), math.log(0.5))), 0.15, 0.5),
        "order": jax.vmap(lambda own: jax.random.permutation(own, PTS_DEV))(jax.random.split(keys[3], DEVICES)).reshape((DEVICES, PTS_DEV)).astype(jnp.int32),
        "leaf_basis": gaussian(keys[4], (NLEAVES, LEAF, R), LEAF ** -0.5, 0.25, ((0, 256),)),
        "leaf_transfer": gaussian(keys[5], (NLEAVES, R, R), R ** -0.5, 0.5, ((0, 256),)),
        "level_transfer": gaussian(keys[6], (N_LEAF, 2 * N_SUB - 2, R, R), R ** -0.5, 0.5, ((0, 8),)),
        "near_list": draw_near_list(jax.random.fold_in(keys[14], 71), 0),
        "near_count": draw_near_count(jax.random.fold_in(keys[14], 71), 0),
        "pair_list": draw_pair_list(jax.random.fold_in(keys[14], 71), 0),
        "pair_count": draw_pair_count(jax.random.fold_in(keys[14], 71), 0),
        "pair_coupling": gaussian(keys[11], (DEVICES, KD, R, R), (R * KD) ** -0.5, 0.3125, ((0, 256),)),
        "top_list": draw_top_list(jax.random.fold_in(keys[14], 71), 0),
        "top_coupling": gaussian(keys[13], (N_LEAF, KS, R, R), (R * KS * N_SUB) ** -0.5, 0.0625, ((0, 8),)),
    }


exact_mode = lax.Precision.HIGHEST


def kernel_tile(rows_scaled, rows_sq, cols_scaled, cols_sq):
    cross = lax.dot_general(rows_scaled, cols_scaled, (((1,), (1,)), ((), ())), preferred_element_type=jnp.float32)
    distance = rows_sq[:, None] + cols_sq[None, :] - 2.0 * cross
    return jnp.exp(-0.5 * distance).astype(jnp.bfloat16)


def reference(points, vectors, inv_length, order, leaf_basis, leaf_transfer, level_transfer, near_list, near_count, pair_list, pair_count, pair_coupling, top_list, top_coupling):
    devices = N_LEAF * N_SUB
    per_dev = LPD * LEAF
    leaves = devices * LPD
    columns = 2 * NV
    levels_count = N_SUB.bit_length() - 1
    starts = jnp.arange(devices, dtype=jnp.int32) * per_dev
    row_order = (order.astype(jnp.int32) + starts[:, None]).reshape(-1)
    ordered = vectors.reshape(devices * per_dev, columns)[row_order]
    scaled = (points[row_order].astype(jnp.float32) * inv_length[None, :]).astype(jnp.bfloat16)
    squares = jnp.sum(jnp.square(scaled.astype(jnp.float32)), axis=1)
    leaf_vals = ordered.reshape(leaves, LEAF, columns)
    scaled_leaf = scaled.reshape(leaves, LEAF, F)
    squares_leaf = squares.reshape(leaves, LEAF)
    leaf_coef = jnp.einsum("lpr,lpw->lrw", leaf_basis.astype(jnp.float32), leaf_vals.astype(jnp.float32), precision=exact_mode)
    lifted = jnp.einsum("lrs,lrw->lsw", leaf_transfer.astype(jnp.float32), leaf_coef, precision=exact_mode)
    node_coef = jnp.sum(lifted.reshape(devices, LPD, R, columns), axis=1)
    level_coef = node_coef.reshape(N_LEAF, N_SUB, R, columns)
    matrices = []
    for depth_step in range(levels_count):
        node_count = N_SUB >> depth_step
        first_node = 2 * N_SUB - 2 * node_count
        matrix = level_transfer[:, first_node:first_node + node_count].astype(jnp.float32)
        matrices.append(matrix)
        lifted_part = jnp.einsum("jnrs,jnrw->jnsw", matrix, level_coef, precision=exact_mode)
        lifted_part = lifted_part.reshape(N_LEAF, node_count // 2, 2, R, columns)
        level_coef = lifted_part[:, :, 0] + lifted_part[:, :, 1]
    top_coef = level_coef[:, 0]
    node_low = node_coef.astype(jnp.bfloat16)
    top_low = top_coef.astype(jnp.bfloat16)

    def pair_one(inputs):
        links, used_count, couplings = inputs
        running = jnp.zeros((R, columns), jnp.float32)
        for member in range(KD):
            product_term = jnp.dot(couplings[member], node_low[links[member]], preferred_element_type=jnp.float32)
            running = running + jnp.where(member < used_count, product_term, 0.0)
        return running

    pair_field = lax.map(pair_one, (pair_list, pair_count, pair_coupling))
    picked = top_low[top_list]
    top_field = jnp.einsum("skrt,sktw->srw", top_coupling.astype(jnp.float32), picked.astype(jnp.float32), precision=exact_mode)
    down_field = top_field[:, None]
    for depth_step in reversed(range(levels_count)):
        down_field = jnp.repeat(down_field, 2, axis=1)
        down_field = jnp.einsum("jnrs,jnsw->jnrw", matrices[depth_step], down_field, precision=exact_mode)
    node_field = down_field.reshape(devices, R, columns) + pair_field
    leaf_field = jnp.einsum("dlrs,dsw->dlrw", leaf_transfer.astype(jnp.float32).reshape(devices, LPD, R, R), node_field, precision=exact_mode)
    leaf_field = leaf_field.reshape(leaves, R, columns).astype(jnp.bfloat16)
    far_sum = jnp.einsum("lpr,lrw->lpw", leaf_basis.astype(jnp.float32), leaf_field.astype(jnp.float32), precision=exact_mode)

    def near_one(inputs):
        leaf_index, near_links, near_used = inputs
        rows_scaled = scaled_leaf[leaf_index]
        rows_sq = squares_leaf[leaf_index]

        def add_member(member, running):
            target = near_links[member]
            tile = kernel_tile(rows_scaled, rows_sq, scaled_leaf[target], squares_leaf[target])
            return running + jnp.dot(tile, leaf_vals[target], preferred_element_type=jnp.float32)

        return lax.fori_loop(jnp.int32(0), near_used, add_member, jnp.zeros((LEAF, columns), jnp.float32))

    near_sum = lax.map(near_one, (jnp.arange(leaves, dtype=jnp.int32), near_list, near_count))
    leaf_sum = far_sum + near_sum
    result = jnp.zeros((devices * per_dev, columns), jnp.float32).at[row_order].set(leaf_sum.reshape(-1, columns))
    return result.reshape(devices * per_dev, 2, NV)
```

```python
import functools

import jax
import jax.numpy as jnp
from jax import lax
from jax.experimental import pallas as pl
from jax.experimental.pallas import tpu as pltpu
from jax.sharding import PartitionSpec as P

REACH = 4
LANES = 128
SUBLANES = 8
VMEM_LIMIT = 60 << 20
UNROLL = 32

bf16 = jnp.bfloat16
f32 = jnp.float32
exact_mode = lax.Precision.HIGHEST

SMEM_SPEC = pl.BlockSpec(memory_space=pltpu.SMEM)
VMEM_SPEC = pl.BlockSpec(memory_space=pltpu.VMEM)


def tn_dot(a, b, precision=None):
    return lax.dot_general(
        a, b, (((0,), (0,)), ((), ())), preferred_element_type=f32, precision=precision
    )


def nt_dot(a, b):
    return lax.dot_general(a, b, (((1,), (1,)), ((), ())), preferred_element_type=f32)


def nn_dot(a, b, precision=None):
    return lax.dot_general(
        a, b, (((1,), (0,)), ((), ())), preferred_element_type=f32, precision=precision
    )


def high_low(x):
    high = x.astype(bf16)
    return high, (x - high.astype(f32)).astype(bf16)


def row_loop(rows, step):
    def several(i, carry):
        for k in range(UNROLL):
            step(i * UNROLL + k)
        return carry

    lax.fori_loop(0, rows // UNROLL, several, 0)


def chunk_loop(rows, size, step):
    def one(i, carry):
        step(pl.ds(pl.multiple_of(i * size, size), size), i)
        return carry

    lax.fori_loop(0, rows // size, one, 0)


def gather_kernel(
    order,
    wanted,
    vectors,
    points,
    inv_length,
    basis,
    transfer,
    m0,
    m1,
    m2,
    m3,
    m4,
    vals_cols,
    rows_aug,
    send,
    path,
    table,
    held_vals,
    held_points,
):
    leaves, leaf_rows, rank = basis.shape
    per_dev, features = points.shape
    width = vectors.shape[1] * vectors.shape[2]

    lane = lax.broadcasted_iota(jnp.int32, (1, LANES), 1)
    is_feature = lane < features
    piece = lane - features
    first, second, third = [(piece == k) | (piece == k + 3) for k in range(3)]

    def augment(r, i):
        x = (points[r, :].astype(f32) * inv_length[...]).astype(bf16).astype(f32)
        table[r, 0:features] = x
        half = -0.5 * jnp.sum(x * x, axis=1, keepdims=True)
        h1 = half.astype(bf16).astype(f32)
        h2 = (half - h1).astype(bf16).astype(f32)
        h3 = half - h1 - h2
        extra = jnp.where(first, h1, jnp.where(second, h2, jnp.where(third, h3, 0.0)))
        table[r, :] = jnp.where(is_feature, table[r, :], extra)

    chunk_loop(per_dev, 256, augment)

    def move(p):
        source = order[0, p]
        held_vals[p] = vectors[source]
        held_points[pl.ds(p, 1), :] = table[pl.ds(source, 1), :]

    row_loop(per_dev, move)

    ones_left = (piece >= 0) & (piece < 3)
    ones_right = (piece >= 3) & (piece < 6)
    node = jnp.zeros((rank, width), f32)
    for leaf in range(leaves):
        base = leaf * leaf_rows

        def spread(r, i):
            start = pl.multiple_of(base + i * 64, 64)
            vals_cols[leaf, r, 0:width] = held_vals[pl.ds(start, 64)].reshape(64, width)
            got = held_points[pl.ds(start, 64), :]
            vals_cols[leaf, r, width : width + LANES] = jnp.where(ones_left, 1.0, got).astype(bf16)
            rows_aug[leaf, r, :] = jnp.where(ones_right, 1.0, got).astype(bf16)

        chunk_loop(leaf_rows, 64, spread)
        coef = tn_dot(basis[leaf], vals_cols[leaf, :, 0:width])
        high, low = high_low(coef)
        node = node + tn_dot(transfer[leaf], high) + tn_dot(transfer[leaf], low)

    product = m0[0, 0].astype(f32)
    for m in (m1, m2, m3, m4):
        product = nn_dot(product, m[0, 0].astype(f32), exact_mode)
    path[...] = product
    lifted = tn_dot(product, node, exact_mode)
    tile_row = lax.broadcasted_iota(jnp.int32, (SUBLANES, LANES), 0)
    request = jnp.zeros((SUBLANES, LANES), f32)
    for k in range(wanted.shape[0]):
        request = jnp.where(tile_row == k, wanted[k].astype(f32), request)
    across = width // LANES
    for c in range(send.shape[0]):
        r, q = (c // across) * SUBLANES, (c % across) * LANES
        send[c, 0] = node[r : r + SUBLANES, q : q + LANES].astype(bf16)
        send[c, 1] = lifted[r : r + SUBLANES, q : q + LANES].astype(bf16)
        send[c, 2] = request.astype(bf16)


def near_kernel(use_before, use_after, rows_aug, vals_cols, before, after, out):
    leaves, leaf_rows, _ = rows_aug.shape
    width = out.shape[2]

    def part(rows, block):
        tile = jnp.exp(nt_dot(rows, block[:, width : width + LANES])).astype(bf16)
        return nn_dot(tile, block[:, 0:width])

    half = leaf_rows // 2
    for leaf in range(leaves):
        left = before[...] if leaf == 0 else vals_cols[leaf - 1]
        right = after[...] if leaf == leaves - 1 else vals_cols[leaf + 1]
        for piece in range(2):
            r = slice(piece * half, piece * half + half)
            rows = rows_aug[leaf, r, :]
            total = part(rows, vals_cols[leaf])
            total = total + use_before[leaf] * part(rows, left)
            total = total + use_after[leaf] * part(rows, right)
            out[leaf, r, :] = total


def root_kernel(received, root):
    total = received[0, 1].astype(f32)
    for j in range(1, received.shape[0]):
        total = total + received[j, 1].astype(f32)
    root[...] = total.astype(bf16)


def choose_kernel(top_list, received, roots, out):
    peers = received.shape[0]
    pairs = out.shape[1] - top_list.shape[1]
    nodes = [received[j, 0] for j in range(peers)]
    tops = [roots[top_list[0, k]] for k in range(top_list.shape[1])]
    for j in range(peers):
        asked = received[j, 2].astype(f32)
        for k in range(pairs):
            offset = jnp.broadcast_to(asked[k : k + 1, :], (SUBLANES, LANES))
            picked = jnp.zeros((SUBLANES, LANES), f32)
            for slot in range(2 * REACH + 1):
                source = j + slot - REACH
                if slot != REACH and 0 <= source < peers:
                    picked = jnp.where(offset == slot, nodes[source].astype(f32), picked)
            out[j, k] = picked.astype(bf16)
        for k, top in enumerate(tops):
            out[j, pairs + k] = top


def final_kernel(
    order,
    pair_count,
    received,
    pair_coupling,
    top_coupling,
    path,
    basis,
    transfer,
    near,
    out,
    held,
):
    leaves, leaf_rows, rank = basis.shape
    width = near.shape[2]
    across = width // LANES
    pairs = pair_coupling.shape[1]
    tops = top_coupling.shape[1]

    def source(k):
        bands = []
        for c in range(0, received.shape[0], across):
            parts = [received[c + q, k].astype(f32) for q in range(across)]
            bands.append(jnp.concatenate(parts, axis=1))
        return jnp.concatenate(bands, axis=0).astype(bf16)

    top_field = jnp.zeros((rank, width), f32)
    for k in range(tops):
        top_field = top_field + nn_dot(top_coupling[0, k], source(pairs + k))
    node_field = nn_dot(path[...], top_field, exact_mode)
    for k in range(pairs):
        term = nn_dot(pair_coupling[0, k], source(k))
        node_field = node_field + jnp.where(k < pair_count[0], term, 0.0)
    high, low = high_low(node_field)
    for leaf in range(leaves):
        field = (nn_dot(transfer[leaf], high) + nn_dot(transfer[leaf], low)).astype(bf16)
        far = nn_dot(basis[leaf], field)
        total = far + near[leaf]
        r = pl.ds(leaf * leaf_rows, leaf_rows)
        for q in range(across):
            held[r, q, :] = total[:, q * LANES : (q + 1) * LANES]

    def move(p):
        out[order[0, p]] = held[p]

    row_loop(leaves * leaf_rows, move)


def exchange(array, axis):
    return lax.all_to_all(array, axis, 0, 0, tiled=True)


def shifted(block, axis, distance):
    devices = range(lax.axis_size(axis))
    route = [(i - distance, i) for i in devices if i - distance in devices]
    return lax.ppermute(block, axis, route)


def call(kernel, args, specs, out_shapes, scratch=(), flops=0, moved=0):
    return pl.pallas_call(
        kernel,
        out_shape=out_shapes,
        in_specs=specs,
        out_specs=jax.tree.map(lambda _: VMEM_SPEC, out_shapes),
        scratch_shapes=list(scratch),
        compiler_params=pltpu.CompilerParams(vmem_limit_bytes=VMEM_LIMIT),
        cost_estimate=pl.CostEstimate(flops=flops, bytes_accessed=moved, transcendentals=0),
    )(*args)


def per_device(
    points,
    vectors,
    inv_length,
    order,
    leaf_basis,
    leaf_transfer,
    level_transfer,
    near_list,
    near_count,
    pair_list,
    pair_count,
    pair_coupling,
    top_list,
    top_coupling,
):
    sub_count = lax.axis_size("sub")
    levels_count = sub_count.bit_length() - 1
    sub_pos = lax.axis_index("sub")
    top_count = lax.axis_size("leaf")
    dev_pos = lax.axis_index("leaf") * sub_count + sub_pos
    leaf_count, leaf_rows, rank = leaf_basis.shape
    per_dev, features = points.shape
    width = vectors.shape[1] * vectors.shape[2]
    pairs = pair_list.shape[1]
    tops = top_list.shape[1]

    wanted = jnp.clip(pair_list[0] - dev_pos + REACH, 0, 2 * REACH)
    matrices = [
        lax.dynamic_slice_in_dim(
            level_transfer,
            2 * sub_count - 2 * (sub_count >> depth) + jnp.right_shift(sub_pos, depth),
            1,
            axis=1,
        )
        for depth in range(levels_count)
    ]
    vals_cols, rows_aug, send, path = call(
        gather_kernel,
        (
            order,
            wanted,
            vectors,
            points,
            inv_length[None],
            leaf_basis,
            leaf_transfer,
            *matrices,
        ),
        [SMEM_SPEC] * 2 + [VMEM_SPEC] * 10,
        (
            jax.ShapeDtypeStruct((leaf_count, leaf_rows, width + LANES), bf16),
            jax.ShapeDtypeStruct((leaf_count, leaf_rows, LANES), bf16),
            jax.ShapeDtypeStruct((sub_count, 3, SUBLANES, LANES), bf16),
            jax.ShapeDtypeStruct((rank, rank), f32),
        ),
        (
            pltpu.VMEM((per_dev, LANES), f32),
            pltpu.VMEM(vectors.shape, bf16),
            pltpu.VMEM((per_dev, LANES), f32),
        ),
        flops=1 << 29,
        moved=1 << 23,
    )

    before = shifted(vals_cols[leaf_count - 1], "sub", 1)
    after = shifted(vals_cols[0], "sub", -1)

    received = exchange(send, "sub")
    tile = jax.ShapeDtypeStruct((SUBLANES, LANES), bf16)
    root = call(root_kernel, (received,), [VMEM_SPEC], tile)
    roots = exchange(jnp.broadcast_to(root[None], (top_count, *root.shape)), "leaf")
    chosen = call(
        choose_kernel,
        (top_list, received, roots),
        [SMEM_SPEC, VMEM_SPEC, VMEM_SPEC],
        jax.ShapeDtypeStruct((sub_count, pairs + tops, SUBLANES, LANES), bf16),
    )
    sources = exchange(chosen, "sub")

    own = dev_pos * leaf_count + jnp.arange(leaf_count, dtype=jnp.int32)[:, None]
    used = jnp.arange(near_list.shape[1], dtype=jnp.int32)[None] < near_count[:, None]
    use_before = jnp.any(used & (near_list == own - 1), axis=1).astype(f32)
    use_after = jnp.any(used & (near_list == own + 1), axis=1).astype(f32)
    near = call(
        near_kernel,
        (use_before, use_after, rows_aug, vals_cols, before, after),
        [SMEM_SPEC] * 2 + [VMEM_SPEC] * 4,
        jax.ShapeDtypeStruct((leaf_count, leaf_rows, width), f32),
        flops=6 << 30,
        moved=1 << 23,
    )

    return call(
        final_kernel,
        (
            order,
            pair_count,
            sources,
            pair_coupling,
            top_coupling,
            path,
            leaf_basis,
            leaf_transfer,
            near,
        ),
        [SMEM_SPEC] * 2 + [VMEM_SPEC] * 7,
        jax.ShapeDtypeStruct(vectors.shape, f32),
        (pltpu.VMEM(vectors.shape, f32),),
        flops=1 << 29,
        moved=1 << 23,
    )


def solution(mesh):
    return jax.shard_map(
        per_device,
        mesh=mesh,
        in_specs=(
            P(("leaf", "sub"), None),
            P(("leaf", "sub"), None, None),
            P(),
            P(("leaf", "sub"), None),
            P(("leaf", "sub"), None, None),
            P(("leaf", "sub"), None, None),
            P("leaf", None, None, None),
            P(("leaf", "sub"), None),
            P(("leaf", "sub")),
            P(("leaf", "sub"), None),
            P(("leaf", "sub")),
            P(("leaf", "sub"), None, None, None),
            P("leaf", None),
            P("leaf", None, None, None),
        ),
        out_specs=P(("leaf", "sub"), None, None),
        check_vma=False,
    )
```

```python
import functools

import jax
import jax.numpy as jnp
from jax import lax
from jax.experimental import pallas as pl
from jax.experimental.pallas import tpu as pltpu
from jax.sharding import PartitionSpec as P

REACH = 4
LANES = 128
SUBLANES = 8
VMEM_LIMIT = 60 << 20
SMALL_LIMIT = 4 << 20
FINAL_LIMIT = 40 << 20
NEAR_LIMIT = 40 << 20
UNROLL = 64
BLOCK = 512
NEAR_GROUPS = ((1, 2, 3), (4, 5, 6, 0, 7))

bf16 = jnp.bfloat16
f32 = jnp.float32
exact_mode = lax.Precision.HIGHEST

SMEM_SPEC = pl.BlockSpec(memory_space=pltpu.SMEM)
VMEM_SPEC = pl.BlockSpec(memory_space=pltpu.VMEM)
ANY_SPEC = pl.BlockSpec(memory_space=pl.ANY)


def tn_dot(a, b, precision=None):
    return lax.dot_general(
        a, b, (((0,), (0,)), ((), ())), preferred_element_type=f32, precision=precision
    )


def nt_dot(a, b):
    return lax.dot_general(a, b, (((1,), (1,)), ((), ())), preferred_element_type=f32)


def nn_dot(a, b, precision=None):
    return lax.dot_general(
        a, b, (((1,), (0,)), ((), ())), preferred_element_type=f32, precision=precision
    )


def high_low(x):
    high = x.astype(bf16)
    return high, (x - high.astype(f32)).astype(bf16)


def row_loop(rows, step):
    def several(i, carry):
        for k in range(UNROLL):
            step(i * UNROLL + k)
        return carry

    lax.fori_loop(0, rows // UNROLL, several, 0)


def chunk_loop(rows, size, step):
    def one(i, carry):
        step(pl.ds(pl.multiple_of(i * size, size), size), i)
        return carry

    lax.fori_loop(0, rows // size, one, 0)


def gather_kernel(
    order,
    position,
    pair_list,
    vectors_hbm,
    points_hbm,
    inv_length,
    basis_hbm,
    transfer_hbm,
    levels_hbm,
    vals_cols_hbm,
    rows_aug_hbm,
    first_hbm,
    last_hbm,
    send,
    path,
    vals_cols,
    rows_aug,
    vectors,
    points,
    basis,
    transfer,
    mats,
    table,
    held_vals,
    held_points,
    sems,
    out_sems,
):
    leaves, leaf_rows, rank = basis.shape
    features, per_dev = points.shape
    width = vectors.shape[1] * vectors.shape[2]
    levels = mats.shape[0]
    sub_count = 1 << levels
    dev_pos, sub_pos = position[0], position[1]

    copies = [
        pltpu.make_async_copy(points_hbm, points, sems.at[0]),
        pltpu.make_async_copy(vectors_hbm, vectors, sems.at[1]),
        pltpu.make_async_copy(basis_hbm, basis, sems.at[2]),
        pltpu.make_async_copy(transfer_hbm, transfer, sems.at[3]),
    ]
    for depth in range(levels):
        node = 2 * sub_count - 2 * (sub_count >> depth) + jnp.right_shift(sub_pos, depth)
        copies.append(
            pltpu.make_async_copy(levels_hbm.at[0, node], mats.at[depth], sems.at[4 + depth])
        )
    for copy in copies:
        copy.start()

    lane = lax.broadcasted_iota(jnp.int32, (1, LANES), 1)
    piece = lane - features

    spare = jnp.zeros((SUBLANES, BLOCK), f32)
    row = lax.broadcasted_iota(jnp.int32, (SUBLANES, BLOCK), 0)
    here = lax.broadcasted_iota(jnp.int32, (features, features), 0)
    there = lax.broadcasted_iota(jnp.int32, (features, features), 1)
    scale = jnp.sum(jnp.where(here == there, inv_length[...], 0.0), axis=1, keepdims=True)

    def augment(r, i):
        x = (points[:, r].astype(f32) * scale).astype(bf16).astype(f32)
        half = -0.5 * jnp.sum(x * x, axis=0, keepdims=True)
        h1 = half.astype(bf16).astype(f32)
        h2 = (half - h1).astype(bf16).astype(f32)
        h3 = half - h1 - h2
        extra = jnp.where(row % 3 == 0, h1, jnp.where(row % 3 == 1, h2, h3))
        extra = jnp.where(row < 6, extra, 0.0)
        pads = [spare] * ((LANES - features) // SUBLANES - 1)
        table[r, :] = jnp.concatenate([x, extra, *pads], axis=0).T

    copies[0].wait()
    chunk_loop(per_dev, BLOCK, augment)

    def move(p):
        source = order[0, p]
        held_vals[p] = vectors[source]
        held_points[pl.ds(p, 1), :] = table[pl.ds(source, 1), :]

    copies[1].wait()
    row_loop(per_dev, move)

    for copy in copies[2:]:
        copy.wait()
    ones_left = (piece >= 0) & (piece < 3)
    ones_right = (piece >= 3) & (piece < 6)
    stores = []
    node = jnp.zeros((rank, width), f32)
    for leaf in range(leaves):
        base = leaf * leaf_rows
        vals = held_vals[base : base + leaf_rows].reshape(leaf_rows, width)
        got = held_points[base : base + leaf_rows, :]
        cols = jnp.where(ones_left, 1.0, got).astype(bf16)
        vals_cols[leaf, :, 0:width] = vals
        vals_cols[leaf, :, width : width + LANES] = cols
        rows_aug[leaf] = jnp.where(ones_right, 1.0, got).astype(bf16)
        places = [
            (vals_cols.at[leaf], vals_cols_hbm.at[leaf], 2 * leaf),
            (rows_aug.at[leaf], rows_aug_hbm.at[leaf], 2 * leaf + 1),
        ]
        if leaf == 0:
            places.append((vals_cols.at[leaf], first_hbm, 2 * leaves))
        if leaf == leaves - 1:
            places.append((vals_cols.at[leaf], last_hbm, 2 * leaves + 1))
        for source, target, slot in places:
            stores.append(pltpu.make_async_copy(source, target, out_sems.at[slot]))
            stores[-1].start()
        coef = tn_dot(basis[leaf], vals)
        high, low = high_low(coef)
        node = node + tn_dot(transfer[leaf], high) + tn_dot(transfer[leaf], low)

    product = mats[0].astype(f32)
    for depth in range(1, levels):
        product = nn_dot(product, mats[depth].astype(f32), exact_mode)
    path[...] = product
    lifted = tn_dot(product, node, exact_mode)
    tile_row = lax.broadcasted_iota(jnp.int32, (SUBLANES, LANES), 0)
    request = jnp.zeros((SUBLANES, LANES), f32)
    for k in range(pair_list.shape[1]):
        offset = jnp.clip(pair_list[0, k] - dev_pos + REACH, 0, 2 * REACH)
        request = jnp.where(tile_row == k, offset.astype(f32), request)
    across = width // LANES
    for c in range(send.shape[0]):
        r, q = (c // across) * SUBLANES, (c % across) * LANES
        send[c, 0] = node[r : r + SUBLANES, q : q + LANES].astype(bf16)
        send[c, 1] = lifted[r : r + SUBLANES, q : q + LANES].astype(bf16)
        send[c, 2] = request.astype(bf16)
    for copy in stores:
        copy.wait()


def near_kernel(members, position, near_list, near_count, rows_hbm, cols_hbm, *rest):
    *edges, out_hbm, rows_aug, vals_cols, ends, out, in_sems, out_sems = rest
    leaves, _, _ = rows_aug.shape
    width = out.shape[2]

    loads = {}

    def want(key, source, target):
        if key not in loads:
            copy = pltpu.make_async_copy(source, target, in_sems.at[len(loads)])
            copy.start()
            loads[key] = [copy, False]

    def block(index):
        if 0 <= index < leaves:
            return ("cols", index), cols_hbm.at[index], vals_cols.at[index]
        side = 0 if index < 0 else 1
        return ("edge", side), edges[side], ends.at[side]

    for leaf in members:
        want(("rows", leaf), rows_hbm.at[leaf], rows_aug.at[leaf])
        for index in (leaf, leaf - 1, leaf + 1):
            want(*block(index))

    def ready(key):
        entry = loads[key]
        if not entry[1]:
            entry[0].wait()
            entry[1] = True

    def flag(leaf, neighbour):
        own = position[0] * leaves + leaf
        found = jnp.int32(0)
        for k in range(near_list.shape[0]):
            hit = (k < near_count[leaf]) & (near_list[k, leaf] == own + neighbour)
            found = found | hit.astype(jnp.int32)
        return found.astype(f32)

    def part(rows, cols):
        tile = jnp.exp(nt_dot(rows, cols[:, width : width + LANES])).astype(bf16)
        return nn_dot(tile, cols[:, 0:width])

    stores = []
    for slot, leaf in enumerate(members):
        ready(("rows", leaf))
        for index in (leaf, leaf - 1, leaf + 1):
            ready(block(index)[0])
        left, right = block(leaf - 1)[2], block(leaf + 1)[2]
        use_left, use_right = flag(leaf, -1), flag(leaf, 1)
        rows = rows_aug[leaf]
        total = part(rows, vals_cols[leaf])
        total = total + use_left * part(rows, left[...])
        total = total + use_right * part(rows, right[...])
        out[slot] = total
        stores.append(pltpu.make_async_copy(out.at[slot], out_hbm.at[slot], out_sems.at[slot]))
        stores[-1].start()
    for copy in stores:
        copy.wait()


def root_kernel(received, roots):
    total = received[0, 1].astype(f32)
    for j in range(1, received.shape[0]):
        total = total + received[j, 1].astype(f32)
    for s in range(roots.shape[0]):
        roots[s] = total.astype(bf16)


def choose_kernel(top_list, received, roots, out):
    peers = received.shape[0]
    pairs = out.shape[1] - top_list.shape[1]
    nodes = [received[j, 0] for j in range(peers)]
    tops = [roots[top_list[0, k]] for k in range(top_list.shape[1])]
    for j in range(peers):
        asked = received[j, 2].astype(f32)
        for k in range(pairs):
            offset = jnp.broadcast_to(asked[k : k + 1, :], (SUBLANES, LANES))
            picked = jnp.zeros((SUBLANES, LANES), f32)
            for slot in range(2 * REACH + 1):
                source = j + slot - REACH
                if slot != REACH and 0 <= source < peers:
                    picked = jnp.where(offset == slot, nodes[source].astype(f32), picked)
            out[j, k] = picked.astype(bf16)
        for k, top in enumerate(tops):
            out[j, pairs + k] = top


def final_kernel(
    order,
    pair_count,
    received,
    pair_hbm,
    top_hbm,
    path_hbm,
    basis_hbm,
    transfer_hbm,
    *rest,
):
    *nears_hbm, out, held, near, pair_coupling, top_coupling, path, basis, transfer, sems = rest
    leaves, leaf_rows, rank = basis.shape
    width = near.shape[2]
    across = width // LANES
    pairs = pair_coupling.shape[1]
    tops = top_coupling.shape[1]

    def load(source, target, slot):
        copy = pltpu.make_async_copy(source, target, sems.at[slot])
        copy.start()
        return copy

    small = [
        load(top_hbm, top_coupling, 0),
        load(pair_hbm, pair_coupling, 1),
        load(transfer_hbm, transfer, 2),
        load(basis_hbm, basis, 3),
        load(path_hbm, path, 4),
    ]
    large = {}
    slots = [(group, i, leaf) for group, m in enumerate(NEAR_GROUPS) for i, leaf in enumerate(m)]
    for group, i, leaf in sorted(slots, key=lambda entry: entry[2]):
        large[leaf] = load(nears_hbm[group].at[i], near.at[leaf], 5 + leaf)

    def source(k):
        bands = []
        for c in range(0, received.shape[0], across):
            parts = [received[c + q, k].astype(f32) for q in range(across)]
            bands.append(jnp.concatenate(parts, axis=1))
        return jnp.concatenate(bands, axis=0).astype(bf16)

    small[0].wait()
    small[1].wait()
    top_field = jnp.zeros((rank, width), f32)
    for k in range(tops):
        top_field = top_field + nn_dot(top_coupling[0, k], source(pairs + k))
    small[4].wait()
    node_field = nn_dot(path[...], top_field, exact_mode)
    for k in range(pairs):
        term = nn_dot(pair_coupling[0, k], source(k))
        node_field = node_field + jnp.where(k < pair_count[0], term, 0.0)
    high, low = high_low(node_field)
    small[2].wait()
    small[3].wait()
    for leaf in range(leaves):
        field = (nn_dot(transfer[leaf], high) + nn_dot(transfer[leaf], low)).astype(bf16)
        far = nn_dot(basis[leaf], field)
        large[leaf].wait()
        total = far + near[leaf]
        r = pl.ds(leaf * leaf_rows, leaf_rows)
        for q in range(across):
            held[r, q, :] = total[:, q * LANES : (q + 1) * LANES]

    def move(p):
        out[order[0, p]] = held[p]

    row_loop(leaves * leaf_rows, move)


def exchange(array, axis):
    return lax.all_to_all(array, axis, 0, 0, tiled=True)


def shifted(block, axis, distance):
    devices = range(lax.axis_size(axis))
    route = [(i - distance, i) for i in devices if i - distance in devices]
    return lax.ppermute(block, axis, route)


def call(kernel, args, specs, outs, scratch=(), out_specs=None, limit=VMEM_LIMIT, flops=0):
    return pl.pallas_call(
        kernel,
        out_shape=outs,
        in_specs=specs,
        out_specs=jax.tree.map(lambda _: VMEM_SPEC, outs) if out_specs is None else out_specs,
        scratch_shapes=list(scratch),
        compiler_params=pltpu.CompilerParams(vmem_limit_bytes=limit),
        cost_estimate=pl.CostEstimate(
            flops=flops, bytes_accessed=flops // 512, transcendentals=0
        ),
    )(*args)


def off_chip(array):
    return pltpu.with_memory_space_constraint(array, pltpu.HBM)


def per_device(
    points,
    vectors,
    inv_length,
    order,
    leaf_basis,
    leaf_transfer,
    level_transfer,
    near_list,
    near_count,
    pair_list,
    pair_count,
    pair_coupling,
    top_list,
    top_coupling,
):
    sub_count = lax.axis_size("sub")
    levels_count = sub_count.bit_length() - 1
    sub_pos = lax.axis_index("sub")
    top_count = lax.axis_size("leaf")
    dev_pos = lax.axis_index("leaf") * sub_count + sub_pos
    leaf_count, leaf_rows, rank = leaf_basis.shape
    per_dev, features = points.shape
    width = vectors.shape[1] * vectors.shape[2]
    pairs = pair_list.shape[1]
    tops = top_list.shape[1]
    position = jnp.stack([dev_pos, sub_pos]).astype(jnp.int32)
    edge = jax.ShapeDtypeStruct((leaf_rows, width + LANES), bf16)

    ext_shape = (leaf_count, leaf_rows, width + LANES)
    aug_shape = (leaf_count, leaf_rows, LANES)
    vals_cols, rows_aug, first_leaf, last_leaf, send, path = call(
        gather_kernel,
        (
            order,
            position,
            pair_list,
            off_chip(vectors),
            off_chip(points.T),
            inv_length[None],
            off_chip(leaf_basis),
            off_chip(leaf_transfer),
            off_chip(level_transfer),
        ),
        [SMEM_SPEC] * 3 + [ANY_SPEC] * 2 + [VMEM_SPEC] + [ANY_SPEC] * 3,
        (
            jax.ShapeDtypeStruct(ext_shape, bf16),
            jax.ShapeDtypeStruct(aug_shape, bf16),
            edge,
            edge,
            jax.ShapeDtypeStruct((sub_count, 3, SUBLANES, LANES), bf16),
            jax.ShapeDtypeStruct((rank, rank), f32),
        ),
        (
            pltpu.VMEM(ext_shape, bf16),
            pltpu.VMEM(aug_shape, bf16),
            pltpu.VMEM(vectors.shape, bf16),
            pltpu.VMEM((features, per_dev), bf16),
            pltpu.VMEM(leaf_basis.shape, bf16),
            pltpu.VMEM(leaf_transfer.shape, bf16),
            pltpu.VMEM((levels_count, rank, rank), bf16),
            pltpu.VMEM((per_dev, LANES), f32),
            pltpu.VMEM(vectors.shape, bf16),
            pltpu.VMEM((per_dev, LANES), f32),
            pltpu.SemaphoreType.DMA((4 + levels_count,)),
            pltpu.SemaphoreType.DMA((2 * leaf_count + 2,)),
        ),
        (ANY_SPEC,) * 4 + (VMEM_SPEC,) * 2,
        flops=1 << 29,
    )

    before = shifted(last_leaf, "sub", 1)
    after = shifted(first_leaf, "sub", -1)

    received = exchange(send, "sub")
    tile = (SUBLANES, LANES)
    own_root = call(
        root_kernel,
        (received,),
        [VMEM_SPEC],
        jax.ShapeDtypeStruct((top_count, *tile), bf16),
        limit=SMALL_LIMIT,
    )
    roots = exchange(own_root, "leaf")
    chosen = call(
        choose_kernel,
        (top_list, received, roots),
        [SMEM_SPEC, VMEM_SPEC, VMEM_SPEC],
        jax.ShapeDtypeStruct((sub_count, pairs + tops, *tile), bf16),
        limit=SMALL_LIMIT,
    )
    sources = exchange(chosen, "sub")

    nears = []
    for members in NEAR_GROUPS:
        needs_edges = 0 in members or leaf_count - 1 in members
        edges = (before, after) if needs_edges else ()
        near_shape = (len(members), leaf_rows, width)
        near = call(
            functools.partial(near_kernel, members),
            (
                off_chip(position),
                near_list.T,
                off_chip(near_count),
                off_chip(rows_aug),
                off_chip(vals_cols),
                *edges,
            ),
            [SMEM_SPEC] * 3 + [ANY_SPEC] * (2 + len(edges)),
            pltpu.HBM(near_shape, f32),
            (
                pltpu.VMEM(aug_shape, bf16),
                pltpu.VMEM(ext_shape, bf16),
                pltpu.VMEM((2, *ext_shape[1:]), bf16),
                pltpu.VMEM(near_shape, f32),
                pltpu.SemaphoreType.DMA((2 * leaf_count + 2,)),
                pltpu.SemaphoreType.DMA((len(members),)),
            ),
            ANY_SPEC,
            limit=NEAR_LIMIT,
            flops=3 << 30,
        )
        nears.append(near)

    return call(
        final_kernel,
        (
            off_chip(order),
            pair_count,
            sources,
            off_chip(pair_coupling),
            off_chip(top_coupling),
            off_chip(path),
            off_chip(leaf_basis),
            off_chip(leaf_transfer),
            *[off_chip(near) for near in nears],
        ),
        [SMEM_SPEC] * 2 + [VMEM_SPEC] + [ANY_SPEC] * (5 + len(nears)),
        jax.ShapeDtypeStruct(vectors.shape, f32),
        (
            pltpu.VMEM(vectors.shape, f32),
            pltpu.VMEM((leaf_count, leaf_rows, width), f32),
            pltpu.VMEM(pair_coupling.shape, bf16),
            pltpu.VMEM(top_coupling.shape, bf16),
            pltpu.VMEM((rank, rank), f32),
            pltpu.VMEM(leaf_basis.shape, bf16),
            pltpu.VMEM(leaf_transfer.shape, bf16),
            pltpu.SemaphoreType.DMA((5 + leaf_count,)),
        ),
        limit=FINAL_LIMIT,
        flops=1 << 29,
    )


def solution(mesh):
    return jax.shard_map(
        per_device,
        mesh=mesh,
        in_specs=(
            P(("leaf", "sub"), None),
            P(("leaf", "sub"), None, None),
            P(),
            P(("leaf", "sub"), None),
            P(("leaf", "sub"), None, None),
            P(("leaf", "sub"), None, None),
            P("leaf", None, None, None),
            P(("leaf", "sub"), None),
            P(("leaf", "sub")),
            P(("leaf", "sub"), None),
            P(("leaf", "sub")),
            P(("leaf", "sub"), None, None, None),
            P("leaf", None),
            P("leaf", None, None, None),
        ),
        out_specs=P(("leaf", "sub"), None, None),
        check_vma=False,
    )
```

```python
import functools

import jax
import jax.numpy as jnp
from jax import lax
from jax.experimental import pallas as pl
from jax.experimental.pallas import tpu as pltpu
from jax.sharding import PartitionSpec as P

REACH = 4
LANES = 128
SUBLANES = 8
VMEM_LIMIT = 60 << 20
SMALL_LIMIT = 4 << 20
FINAL_LIMIT = 40 << 20
NEAR_LIMIT = 40 << 20
BLOCK = 512
NEAR_GROUPS = ((1, 2, 3), (4, 5, 6, 0, 7))

bf16 = jnp.bfloat16
f32 = jnp.float32
exact_mode = lax.Precision.HIGHEST

SMEM_SPEC = pl.BlockSpec(memory_space=pltpu.SMEM)
VMEM_SPEC = pl.BlockSpec(memory_space=pltpu.VMEM)
ANY_SPEC = pl.BlockSpec(memory_space=pl.ANY)


def tn_dot(a, b, precision=None):
    return lax.dot_general(
        a, b, (((0,), (0,)), ((), ())), preferred_element_type=f32, precision=precision
    )


def nt_dot(a, b):
    return lax.dot_general(a, b, (((1,), (1,)), ((), ())), preferred_element_type=f32)


def nn_dot(a, b, precision=None):
    return lax.dot_general(
        a, b, (((1,), (0,)), ((), ())), preferred_element_type=f32, precision=precision
    )


def high_low(x):
    high = x.astype(bf16)
    return high, (x - high.astype(f32)).astype(bf16)


def chunk_loop(rows, size, step):
    def one(i, carry):
        step(pl.ds(pl.multiple_of(i * size, size), size), i)
        return carry

    lax.fori_loop(0, rows // size, one, 0)


def gather_kernel(
    order,
    position,
    pair_list,
    vectors_hbm,
    points_hbm,
    inv_length,
    basis_hbm,
    transfer_hbm,
    levels_hbm,
    vals_cols_hbm,
    rows_aug_hbm,
    first_hbm,
    last_hbm,
    send,
    path,
    vals_cols,
    rows_aug,
    vectors,
    points,
    basis,
    transfer,
    mats,
    table,
    held_vals,
    held_points,
    sems,
    out_sems,
    edge_sems,
):
    leaves, leaf_rows, rank = basis.shape
    features, per_dev = points.shape
    width = vectors.shape[1] * vectors.shape[2]
    levels = mats.shape[0]
    sub_count = 1 << levels
    dev_pos, sub_pos = position[0], position[1]

    copies = [
        pltpu.make_async_copy(points_hbm, points, sems.at[0]),
        pltpu.make_async_copy(vectors_hbm, vectors, sems.at[1]),
        pltpu.make_async_copy(basis_hbm, basis, sems.at[2]),
        pltpu.make_async_copy(transfer_hbm, transfer, sems.at[3]),
    ]
    for depth in range(levels):
        node = 2 * sub_count - 2 * (sub_count >> depth) + jnp.right_shift(sub_pos, depth)
        copies.append(
            pltpu.make_async_copy(levels_hbm.at[0, node], mats.at[depth], sems.at[4 + depth])
        )
    for copy in copies:
        copy.start()

    lane = lax.broadcasted_iota(jnp.int32, (1, LANES), 1)
    piece = lane - features

    spare = jnp.zeros((SUBLANES, BLOCK), f32)
    row = lax.broadcasted_iota(jnp.int32, (SUBLANES, BLOCK), 0)
    here = lax.broadcasted_iota(jnp.int32, (features, features), 0)
    there = lax.broadcasted_iota(jnp.int32, (features, features), 1)
    scale = jnp.sum(jnp.where(here == there, inv_length[...], 0.0), axis=1, keepdims=True)

    def augment(r, i):
        x = (points[:, r].astype(f32) * scale).astype(bf16).astype(f32)
        half = -0.5 * jnp.sum(x * x, axis=0, keepdims=True)
        h1 = half.astype(bf16).astype(f32)
        h2 = (half - h1).astype(bf16).astype(f32)
        h3 = half - h1 - h2
        extra = jnp.where(row % 3 == 0, h1, jnp.where(row % 3 == 1, h2, h3))
        extra = jnp.where(row < 6, extra, 0.0)
        pads = [spare] * ((LANES - features) // SUBLANES - 1)
        table[r, :] = jnp.concatenate([x, extra, *pads], axis=0).T

    copies[0].wait()
    chunk_loop(per_dev, BLOCK, augment)

    def move_leaf(leaf):
        start = pl.multiple_of(leaf * leaf_rows, leaf_rows)
        for k in range(leaf_rows):
            source = order[0, start + k]
            held_vals[start + k] = vectors[source]
            held_points[pl.ds(start + k, 1), :] = table[pl.ds(source, 1), :]

    for copy in copies[1:]:
        copy.wait()
    ones_left = (piece >= 0) & (piece < 3)
    ones_right = (piece >= 3) & (piece < 6)

    def stores_of(leaf):
        return [
            pltpu.make_async_copy(vals_cols.at[leaf], vals_cols_hbm.at[leaf], out_sems.at[leaf, 0]),
            pltpu.make_async_copy(rows_aug.at[leaf], rows_aug_hbm.at[leaf], out_sems.at[leaf, 1]),
        ]

    def form(leaf):
        start = pl.multiple_of(leaf * leaf_rows, leaf_rows)
        vals = held_vals[pl.ds(start, leaf_rows)].reshape(leaf_rows, width)
        got = held_points[pl.ds(start, leaf_rows), :]
        cols = jnp.where(ones_left, 1.0, got).astype(bf16)
        vals_cols[leaf, :, 0:width] = vals
        vals_cols[leaf, :, width : width + LANES] = cols
        rows_aug[leaf] = jnp.where(ones_right, 1.0, got).astype(bf16)
        coef = tn_dot(basis[leaf], vals)
        high, low = high_low(coef)
        return tn_dot(transfer[leaf], high) + tn_dot(transfer[leaf], low)

    def one_leaf(leaf, total):
        total = total + form(leaf)
        move_leaf(leaf + 1)
        for copy in stores_of(leaf):
            copy.start()
        return total

    move_leaf(0)
    last = leaves - 1
    node = lax.fori_loop(0, last, one_leaf, jnp.zeros((rank, width), f32))
    node = node + form(last)
    edges = [
        pltpu.make_async_copy(vals_cols.at[0], first_hbm, edge_sems.at[0]),
        pltpu.make_async_copy(vals_cols.at[last], last_hbm, edge_sems.at[1]),
    ]
    for copy in stores_of(last) + edges:
        copy.start()

    product = mats[0].astype(f32)
    for depth in range(1, levels):
        product = nn_dot(product, mats[depth].astype(f32), exact_mode)
    path[...] = product
    lifted = tn_dot(product, node, exact_mode)
    tile_row = lax.broadcasted_iota(jnp.int32, (SUBLANES, LANES), 0)
    request = jnp.zeros((SUBLANES, LANES), f32)
    for k in range(pair_list.shape[1]):
        offset = jnp.clip(pair_list[0, k] - dev_pos + REACH, 0, 2 * REACH)
        request = jnp.where(tile_row == k, offset.astype(f32), request)
    across = width // LANES
    for c in range(send.shape[0]):
        r, q = (c // across) * SUBLANES, (c % across) * LANES
        send[c, 0] = node[r : r + SUBLANES, q : q + LANES].astype(bf16)
        send[c, 1] = lifted[r : r + SUBLANES, q : q + LANES].astype(bf16)
        send[c, 2] = request.astype(bf16)
    for leaf in range(leaves):
        for copy in stores_of(leaf):
            copy.wait()
    for copy in edges:
        copy.wait()


def near_kernel(members, position, near_list, near_count, rows_hbm, cols_hbm, *rest):
    *edges, out_hbm, rows_aug, vals_cols, ends, out, in_sems, out_sems = rest
    leaves, _, _ = rows_aug.shape
    width = out.shape[2]

    loads = {}

    def want(key, source, target):
        if key not in loads:
            copy = pltpu.make_async_copy(source, target, in_sems.at[len(loads)])
            copy.start()
            loads[key] = [copy, False]

    def block(index):
        if 0 <= index < leaves:
            return ("cols", index), cols_hbm.at[index], vals_cols.at[index]
        side = 0 if index < 0 else 1
        return ("edge", side), edges[side], ends.at[side]

    for leaf in members:
        want(("rows", leaf), rows_hbm.at[leaf], rows_aug.at[leaf])
        for index in (leaf, leaf - 1, leaf + 1):
            want(*block(index))

    def ready(key):
        entry = loads[key]
        if not entry[1]:
            entry[0].wait()
            entry[1] = True

    def flag(leaf, neighbour):
        own = position[0] * leaves + leaf
        found = jnp.int32(0)
        for k in range(near_list.shape[0]):
            hit = (k < near_count[leaf]) & (near_list[k, leaf] == own + neighbour)
            found = found | hit.astype(jnp.int32)
        return found.astype(f32)

    def part(rows, cols):
        tile = jnp.exp(nt_dot(rows, cols[:, width : width + LANES])).astype(bf16)
        return nn_dot(tile, cols[:, 0:width])

    stores = []
    for slot, leaf in enumerate(members):
        ready(("rows", leaf))
        for index in (leaf, leaf - 1, leaf + 1):
            ready(block(index)[0])
        left, right = block(leaf - 1)[2], block(leaf + 1)[2]
        use_left, use_right = flag(leaf, -1), flag(leaf, 1)
        rows = rows_aug[leaf]
        total = part(rows, vals_cols[leaf])
        total = total + use_left * part(rows, left[...])
        total = total + use_right * part(rows, right[...])
        out[slot] = total
        stores.append(pltpu.make_async_copy(out.at[slot], out_hbm.at[slot], out_sems.at[slot]))
        stores[-1].start()
    for copy in stores:
        copy.wait()


def root_kernel(received, roots):
    total = received[0, 1].astype(f32)
    for j in range(1, received.shape[0]):
        total = total + received[j, 1].astype(f32)
    for s in range(roots.shape[0]):
        roots[s] = total.astype(bf16)


def choose_kernel(top_list, received, roots, out):
    peers = received.shape[0]
    pairs = out.shape[1] - top_list.shape[1]
    nodes = [received[j, 0] for j in range(peers)]
    tops = [roots[top_list[0, k]] for k in range(top_list.shape[1])]
    for j in range(peers):
        asked = received[j, 2].astype(f32)
        for k in range(pairs):
            offset = jnp.broadcast_to(asked[k : k + 1, :], (SUBLANES, LANES))
            picked = jnp.zeros((SUBLANES, LANES), f32)
            for slot in range(2 * REACH + 1):
                source = j + slot - REACH
                if slot != REACH and 0 <= source < peers:
                    picked = jnp.where(offset == slot, nodes[source].astype(f32), picked)
            out[j, k] = picked.astype(bf16)
        for k, top in enumerate(tops):
            out[j, pairs + k] = top


def final_kernel(
    order,
    pair_count,
    received,
    pair_hbm,
    top_hbm,
    path_hbm,
    basis_hbm,
    transfer_hbm,
    *rest,
):
    *nears_hbm, out, held, near, pair_coupling, top_coupling, path, basis, transfer, sems = rest
    leaves, leaf_rows, rank = basis.shape
    width = near.shape[2]
    across = width // LANES
    pairs = pair_coupling.shape[1]
    tops = top_coupling.shape[1]

    def load(source, target, slot):
        copy = pltpu.make_async_copy(source, target, sems.at[slot])
        copy.start()
        return copy

    small = [
        load(top_hbm, top_coupling, 0),
        load(pair_hbm, pair_coupling, 1),
        load(transfer_hbm, transfer, 2),
        load(basis_hbm, basis, 3),
        load(path_hbm, path, 4),
    ]
    large = {}
    slots = [(group, i, leaf) for group, m in enumerate(NEAR_GROUPS) for i, leaf in enumerate(m)]
    for group, i, leaf in sorted(slots, key=lambda entry: entry[2]):
        large[leaf] = load(nears_hbm[group].at[i], near.at[leaf], 5 + leaf)

    def source(k):
        bands = []
        for c in range(0, received.shape[0], across):
            parts = [received[c + q, k].astype(f32) for q in range(across)]
            bands.append(jnp.concatenate(parts, axis=1))
        return jnp.concatenate(bands, axis=0).astype(bf16)

    small[0].wait()
    small[1].wait()
    top_field = jnp.zeros((rank, width), f32)
    for k in range(tops):
        top_field = top_field + nn_dot(top_coupling[0, k], source(pairs + k))
    small[4].wait()
    node_field = nn_dot(path[...], top_field, exact_mode)
    for k in range(pairs):
        term = nn_dot(pair_coupling[0, k], source(k))
        node_field = node_field + jnp.where(k < pair_count[0], term, 0.0)
    high, low = high_low(node_field)
    small[2].wait()
    small[3].wait()
    for leaf in range(leaves):
        large[leaf].wait()

    def move_leaf(leaf):
        start = pl.multiple_of(leaf * leaf_rows, leaf_rows)
        for k in range(leaf_rows):
            out[order[0, start + k]] = held[start + k]

    def form(leaf):
        field = (nn_dot(transfer[leaf], high) + nn_dot(transfer[leaf], low)).astype(bf16)
        total = nn_dot(basis[leaf], field) + near[leaf]
        r = pl.ds(pl.multiple_of(leaf * leaf_rows, leaf_rows), leaf_rows)
        for q in range(across):
            held[r, q, :] = total[:, q * LANES : (q + 1) * LANES]

    def one_leaf(leaf, carry):
        move_leaf(leaf - 1)
        form(leaf)
        return carry

    form(0)
    lax.fori_loop(1, leaves, one_leaf, 0)
    move_leaf(leaves - 1)


def exchange(array, axis):
    return lax.all_to_all(array, axis, 0, 0, tiled=True)


def shifted(block, axis, distance):
    devices = range(lax.axis_size(axis))
    route = [(i - distance, i) for i in devices if i - distance in devices]
    return lax.ppermute(block, axis, route)


def call(kernel, args, specs, outs, scratch=(), out_specs=None, limit=VMEM_LIMIT, flops=0):
    return pl.pallas_call(
        kernel,
        out_shape=outs,
        in_specs=specs,
        out_specs=jax.tree.map(lambda _: VMEM_SPEC, outs) if out_specs is None else out_specs,
        scratch_shapes=list(scratch),
        compiler_params=pltpu.CompilerParams(vmem_limit_bytes=limit),
        cost_estimate=pl.CostEstimate(
            flops=flops, bytes_accessed=flops // 512, transcendentals=0
        ),
    )(*args)


def off_chip(array):
    return pltpu.with_memory_space_constraint(array, pltpu.HBM)


def per_device(
    points,
    vectors,
    inv_length,
    order,
    leaf_basis,
    leaf_transfer,
    level_transfer,
    near_list,
    near_count,
    pair_list,
    pair_count,
    pair_coupling,
    top_list,
    top_coupling,
):
    sub_count = lax.axis_size("sub")
    levels_count = sub_count.bit_length() - 1
    sub_pos = lax.axis_index("sub")
    top_count = lax.axis_size("leaf")
    dev_pos = lax.axis_index("leaf") * sub_count + sub_pos
    leaf_count, leaf_rows, rank = leaf_basis.shape
    per_dev, features = points.shape
    width = vectors.shape[1] * vectors.shape[2]
    pairs = pair_list.shape[1]
    tops = top_list.shape[1]
    position = jnp.stack([dev_pos, sub_pos]).astype(jnp.int32)
    edge = jax.ShapeDtypeStruct((leaf_rows, width + LANES), bf16)

    ext_shape = (leaf_count, leaf_rows, width + LANES)
    aug_shape = (leaf_count, leaf_rows, LANES)
    vals_cols, rows_aug, first_leaf, last_leaf, send, path = call(
        gather_kernel,
        (
            order,
            position,
            pair_list,
            off_chip(vectors),
            off_chip(points.T),
            inv_length[None],
            off_chip(leaf_basis),
            off_chip(leaf_transfer),
            off_chip(level_transfer),
        ),
        [SMEM_SPEC] * 3 + [ANY_SPEC] * 2 + [VMEM_SPEC] + [ANY_SPEC] * 3,
        (
            jax.ShapeDtypeStruct(ext_shape, bf16),
            jax.ShapeDtypeStruct(aug_shape, bf16),
            edge,
            edge,
            jax.ShapeDtypeStruct((sub_count, 3, SUBLANES, LANES), bf16),
            jax.ShapeDtypeStruct((rank, rank), f32),
        ),
        (
            pltpu.VMEM(ext_shape, bf16),
            pltpu.VMEM(aug_shape, bf16),
            pltpu.VMEM(vectors.shape, bf16),
            pltpu.VMEM((features, per_dev), bf16),
            pltpu.VMEM(leaf_basis.shape, bf16),
            pltpu.VMEM(leaf_transfer.shape, bf16),
            pltpu.VMEM((levels_count, rank, rank), bf16),
            pltpu.VMEM((per_dev, LANES), f32),
            pltpu.VMEM(vectors.shape, bf16),
            pltpu.VMEM((per_dev, LANES), f32),
            pltpu.SemaphoreType.DMA((4 + levels_count,)),
            pltpu.SemaphoreType.DMA((leaf_count, 2)),
            pltpu.SemaphoreType.DMA((2,)),
        ),
        (ANY_SPEC,) * 4 + (VMEM_SPEC,) * 2,
        flops=1 << 29,
    )

    before = shifted(last_leaf, "sub", 1)
    after = shifted(first_leaf, "sub", -1)

    received = exchange(send, "sub")
    tile = (SUBLANES, LANES)
    own_root = call(
        root_kernel,
        (received,),
        [VMEM_SPEC],
        jax.ShapeDtypeStruct((top_count, *tile), bf16),
        limit=SMALL_LIMIT,
    )
    roots = exchange(own_root, "leaf")
    chosen = call(
        choose_kernel,
        (top_list, received, roots),
        [SMEM_SPEC, VMEM_SPEC, VMEM_SPEC],
        jax.ShapeDtypeStruct((sub_count, pairs + tops, *tile), bf16),
        limit=SMALL_LIMIT,
    )
    sources = exchange(chosen, "sub")

    nears = []
    for members in NEAR_GROUPS:
        needs_edges = 0 in members or leaf_count - 1 in members
        edges = (before, after) if needs_edges else ()
        near_shape = (len(members), leaf_rows, width)
        near = call(
            functools.partial(near_kernel, members),
            (
                off_chip(position),
                near_list.T,
                off_chip(near_count),
                off_chip(rows_aug),
                off_chip(vals_cols),
                *edges,
            ),
            [SMEM_SPEC] * 3 + [ANY_SPEC] * (2 + len(edges)),
            pltpu.HBM(near_shape, f32),
            (
                pltpu.VMEM(aug_shape, bf16),
                pltpu.VMEM(ext_shape, bf16),
                pltpu.VMEM((2, *ext_shape[1:]), bf16),
                pltpu.VMEM(near_shape, f32),
                pltpu.SemaphoreType.DMA((2 * leaf_count + 2,)),
                pltpu.SemaphoreType.DMA((len(members),)),
            ),
            ANY_SPEC,
            limit=NEAR_LIMIT,
            flops=3 << 30,
        )
        nears.append(near)

    return call(
        final_kernel,
        (
            off_chip(order),
            pair_count,
            sources,
            off_chip(pair_coupling),
            off_chip(top_coupling),
            off_chip(path),
            off_chip(leaf_basis),
            off_chip(leaf_transfer),
            *[off_chip(near) for near in nears],
        ),
        [SMEM_SPEC] * 2 + [VMEM_SPEC] + [ANY_SPEC] * (5 + len(nears)),
        jax.ShapeDtypeStruct(vectors.shape, f32),
        (
            pltpu.VMEM(vectors.shape, f32),
            pltpu.VMEM((leaf_count, leaf_rows, width), f32),
            pltpu.VMEM(pair_coupling.shape, bf16),
            pltpu.VMEM(top_coupling.shape, bf16),
            pltpu.VMEM((rank, rank), f32),
            pltpu.VMEM(leaf_basis.shape, bf16),
            pltpu.VMEM(leaf_transfer.shape, bf16),
            pltpu.SemaphoreType.DMA((5 + leaf_count,)),
        ),
        limit=FINAL_LIMIT,
        flops=1 << 29,
    )


def solution(mesh):
    return jax.shard_map(
        per_device,
        mesh=mesh,
        in_specs=(
            P(("leaf", "sub"), None),
            P(("leaf", "sub"), None, None),
            P(),
            P(("leaf", "sub"), None),
            P(("leaf", "sub"), None, None),
            P(("leaf", "sub"), None, None),
            P("leaf", None, None, None),
            P(("leaf", "sub"), None),
            P(("leaf", "sub")),
            P(("leaf", "sub"), None),
            P(("leaf", "sub")),
            P(("leaf", "sub"), None, None, None),
            P("leaf", None),
            P("leaf", None, None, None),
        ),
        out_specs=P(("leaf", "sub"), None, None),
        check_vma=False,
    )
```
